256 devices in a mesh: node: 16 (over x_lo, z), shard: 16 (over x_hi, y, core).
Axes of the slice: x: 4 (x_hi: 2, x_lo: 2; x = x_hi * 2 + x_lo), y: 4, z: 8, core: 2. Of those that a mesh axis runs over, the one named last changes fastest.
Arguments:
- hidden: bfloat16 [16, 2048, 7168], P('node', 'shard'), may hold values from -6 to 6
- cotangent: bfloat16 [16, 2048, 2048], P('node', 'shard'), may hold values from -0.125 to 0.125
- weights: bfloat16 [16, 7168, 2048], P('node', 'shard'), may hold values from -0.59765625 to 0.59765625
- momentum: bfloat16 [16, 7168, 2048], P('node', 'shard'), may hold values from -6 to 6
Outputs:
- new_weights: bfloat16 [16, 7168, 2048], P('node', 'shard')
- new_momentum: bfloat16 [16, 7168, 2048], P('node', 'shard')
The draws below stay inside these ranges and needn't reach their ends.
All inputs are finite; a program needn't handle non-finite values.
Results may differ from the reference program's by a relative error of at most 0.0085.
Values may be sent and summed in bfloat16 or wider, within the bound.
No kernel may reach another device: no remote copies, remote signals or barrier semaphores. Data moves between devices by JAX's collectives and lax.ppermute only.
A program may use at most 64 MiB of HBM per device.

```python
import jax
import jax.numpy as jnp
from jax import lax

FFW = 7168
DW = 2048
TOKENS = 2048
NODES = 16
N_NODE = 16


def steps_of(rng, extent, split, least, top_value):
    gain, own = 1.0, jax.random.fold_in(rng, 6)
    for position, parts in split:
        heights = jnp.exp(jax.random.uniform(jax.random.fold_in(own, position), (parts,), jnp.float32, least / len(split), top_value / len(split)))
        gain = gain * jnp.repeat(heights, extent[position] // parts).reshape([-1 if axis == position else 1 for axis in range(len(extent))])
    return gain


def normal_values(stream_key, extent, deviation, most, pieces=(), kind=jnp.bfloat16):
    gain = steps_of(stream_key, extent, pieces, -0.22, 0.18) if pieces else 1.0
    drawn = jax.random.normal(stream_key, extent, jnp.float32) * deviation * gain
    return jnp.minimum(jnp.maximum(drawn, -most), most).astype(kind)


def setup_inputs(seed: int = 0) -> dict:
    streams_of = jax.random.split(jax.random.key(seed), 5)
    return {
        "hidden": normal_values(streams_of[0], (NODES, TOKENS, FFW), 1.0, 6.0, ((0, 16), (1, 16))),
        "cotangent": normal_values(streams_of[1], (NODES, TOKENS, DW), TOKENS ** -0.5, 0.125, ((0, 16), (1, 16))),
        "weights": normal_values(streams_of[2], (NODES, FFW, DW), 0.1, 0.59765625, ((0, 16), (1, 16))),
        "momentum": normal_values(streams_of[3], (NODES, FFW, DW), 1.0, 6.0, ((0, 16), (1, 16))),
    }


step_size = 0.1
friction = 0.9


def reference(hidden, cotangent, weights, momentum):
    node_ids = jnp.arange(N_NODE, dtype=jnp.int32)

    def update(node):
        gradient = lax.dot_general(hidden[node], cotangent[node], (((0,), (0,)), ((), ())), preferred_element_type=jnp.float32)
        new_moment = (friction * momentum[node].astype(jnp.float32) + gradient).astype(jnp.bfloat16)
        kept = lax.optimization_barrier(new_moment)
        half_step = (weights[node].astype(jnp.float32) - step_size * kept.astype(jnp.float32)).astype(jnp.bfloat16)
        return new_moment, half_step

    moment_all, half_all = lax.map(update, node_ids)
    half_all = lax.optimization_barrier(half_all)
    row_count = N_NODE // 4

    def trimmed(node):
        row_pos = node // 4
        col_pos = node % 4
        others = [node,
                  row_pos * 4 + (col_pos + 1) % 4,
                  row_pos * 4 + (col_pos + 3) % 4,
                  ((row_pos + 1) % row_count) * 4 + col_pos,
                  ((row_pos + row_count - 1) % row_count) * 4 + col_pos]
        candidates = [half_all[other].astype(jnp.float32) for other in others]
        running = candidates[0]
        largest = candidates[0]
        smallest = candidates[0]
        for value in candidates[1:]:
            running = running + value
            largest = jnp.maximum(largest, value)
            smallest = jnp.minimum(smallest, value)
        return ((running - largest - smallest) / 3.0).astype(jnp.bfloat16)

    new_weights = lax.map(trimmed, node_ids)
    return new_weights, moment_all
```

```python
import functools
import jax
import jax.numpy as jnp
from jax import lax
from jax.experimental import pallas as pl
from jax.experimental.pallas import tpu as pltpu
from jax.sharding import PartitionSpec as P

step_size = 0.1
friction = 0.9
CHUNKS = 2
NODES = 16
CORE_GROUPS = [[0, 2, 4, 6, 8, 10, 12, 14], [1, 3, 5, 7, 9, 11, 13, 15]]


def shard_move(value, target):
    return lax.ppermute(value, "shard", [(s, target(s)) for s in range(16)])


def other_hi(s):
    return s ^ 8


def other_core(s):
    return s ^ 1


def along_y(s, step):
    return (s & 9) | ((s + 2 * step) & 6)


def partial_kernel(flip, acts, *refs):
    grads, (out,) = refs[:8], refs[8:]
    rows = out.shape[0]
    here = lax.axis_index("shard")
    start = pl.multiple_of(((here & 1) ^ flip) * rows, 64)
    slots = [((here >> 3) ^ far) * 4 + (((here >> 1) + up) & 3) for up in (0, 3, 1, 2) for far in (0, 1)]
    lhs = jnp.concatenate([acts[slot, pl.ds(start, rows), :] for slot in slots], axis=1)
    rhs = jnp.concatenate([g[...] for g in grads], axis=0)
    out[...] = jnp.dot(lhs, rhs, preferred_element_type=jnp.float32).astype(out.dtype)


def partial_sum(flip, acts, grads, dtype):
    rows, cols = acts.shape[1] // 2, grads[0].shape[1]
    tile = 256
    return pl.pallas_call(
        functools.partial(partial_kernel, flip),
        grid=(cols // tile,),
        in_specs=[pl.BlockSpec(acts.shape, lambda j: (0, 0, 0))]
        + [pl.BlockSpec((g.shape[0], tile), lambda j: (0, j)) for g in grads],
        out_specs=pl.BlockSpec((rows, tile), lambda j: (0, j)),
        out_shape=jax.ShapeDtypeStruct((rows, cols), dtype),
        name="partial_sum",
    )(acts, *grads)


def step_kernel(own, other, weights, moment, *refs):
    new_moment, half = refs[-2:]
    grad = own[...] + other[...].astype(jnp.float32)
    moved = (friction * moment[...].astype(jnp.float32) + grad).astype(jnp.bfloat16)
    new_moment[...] = moved
    stepped = (weights[...].astype(jnp.float32) - step_size * moved.astype(jnp.float32)).astype(jnp.bfloat16)
    bands, rows = half.shape[0], half.shape[2]
    for b in range(bands):
        half[b, 0] = stepped[b * rows : (b + 1) * rows]


def step(own, other, weights, moment, carried, chunk):
    rows, cols = own.shape
    total = weights.shape[1]
    bands = NODES * 128 // cols
    blocks = cols // 128
    first = chunk * blocks
    at = pl.BlockSpec((rows, 128), lambda j: (0, j))
    there = pl.BlockSpec((rows, 128), lambda j: (0, first + j))
    extra = [] if carried is None else [carried]
    return pl.pallas_call(
        step_kernel,
        grid=(blocks,),
        in_specs=[at, at, there, there] + [pl.BlockSpec(memory_space=pl.ANY)] * len(extra),
        out_specs=[there, pl.BlockSpec((bands, 1, rows // bands, 128), lambda j: (0, j, 0, 0))],
        out_shape=[
            jax.ShapeDtypeStruct((rows, total), jnp.bfloat16),
            jax.ShapeDtypeStruct((bands, blocks, rows // bands, 128), jnp.bfloat16),
        ],
        input_output_aliases={4: 0} if extra else {},
        name="step",
    )(own, other, weights, moment, *extra)


def trim_kernel(halves, out):
    def load(r, c):
        return halves[4 * r + c].astype(jnp.float32)

    values = [[load(r, c) for c in range(4)] for r in range(4)]

    def pair(a, b):
        return a + b, jnp.maximum(a, b), jnp.minimum(a, b)

    beside = [[pair(values[r][1 - q], values[r][3 - q]) for q in range(2)] for r in range(4)]
    above = [[pair(values[1 - q][c], values[3 - q][c]) for c in range(4)] for q in range(2)]
    for r in range(4):
        for c in range(4):
            s = values[r][c]
            cs, cmax, cmin = beside[r][c % 2]
            rs, rmax, rmin = above[r % 2][c]
            largest = jnp.maximum(jnp.maximum(cmax, rmax), s)
            smallest = jnp.minimum(jnp.minimum(cmin, rmin), s)
            out[4 * r + c] = ((s + cs + rs - largest - smallest) / 3.0).astype(out.dtype)


def trim(halves):
    nodes, rows, lanes = halves.shape
    tile = 16
    spec = pl.BlockSpec((nodes, rows // 7, lanes), lambda i: (0, i, 0))
    return pl.pallas_call(
        trim_kernel,
        grid=(7,),
        in_specs=[spec],
        out_specs=spec,
        out_shape=jax.ShapeDtypeStruct(halves.shape, halves.dtype),
        name="trim",
    )(halves)


def gather_kernel(*refs):
    out = refs[-1]
    blocks = out.shape[1] // 128
    per = blocks // (len(refs) - 1)
    for k, piece in enumerate(refs[:-1]):
        bands, rows = NODES // per, piece.shape[1]
        for b in range(bands):
            for j in range(per):
                lane = (k * per + j) * 128
                out[b * rows : (b + 1) * rows, lane : lane + 128] = piece[b * per + j]


def assemble(pieces, shape):
    return pl.pallas_call(
        gather_kernel,
        out_shape=jax.ShapeDtypeStruct(shape, jnp.bfloat16),
        name="assemble",
    )(*pieces)


def on_device(hidden, cotangent, weights, momentum):
    acts, grads, weights, moment = hidden[0], cotangent[0], weights[0], momentum[0]
    acts = acts.T.reshape(8, 896, 128)
    acts = lax.all_to_all(acts, "shard", split_axis=0, concat_axis=0, axis_index_groups=CORE_GROUPS)

    width = grads.shape[1] // CHUNKS
    pieces = []
    for k in range(CHUNKS):
        own = grads[:, k * width : (k + 1) * width]
        far = shard_move(own, other_hi)
        from_below = [shard_move(v, lambda s: along_y(s, 1)) for v in (own, far)]
        from_above = [shard_move(v, lambda s: along_y(s, -1)) for v in (own, far)]
        opposite = [
            shard_move(from_below[0], lambda s: along_y(s, 1)),
            shard_move(from_above[1], lambda s: along_y(s, -1)),
        ]
        pieces.append([own, far, *from_below, *from_above, *opposite])

    new_moment = None
    back = []
    for k in range(CHUNKS):
        sent = partial_sum(1, acts, pieces[k], jnp.bfloat16)
        other = shard_move(sent, other_core)
        own = partial_sum(0, acts, pieces[k], jnp.float32)
        new_moment, half = step(own, other, weights, moment, new_moment, k)
        half = half.reshape(NODES, -1, 128)
        halves = lax.all_to_all(half, "node", split_axis=0, concat_axis=0)
        trimmed = trim(halves)
        back.append(lax.all_to_all(trimmed, "node", split_axis=0, concat_axis=0))
    new_weights = assemble(back, weights.shape)
    return new_weights[None], new_moment[None]


def solution(mesh):
    spec = P("node", "shard", None)
    return jax.shard_map(on_device, mesh=mesh, in_specs=(spec,) * 4, out_specs=(spec, spec), check_vma=False)
```

```python
import functools
import jax
import jax.numpy as jnp
from jax import lax
from jax.experimental import pallas as pl
from jax.sharding import PartitionSpec as P

step_size = 0.1
friction = 0.9
BLOCKS = (6, 10)
NODES = 16
LANES = 128
CORE_GROUPS = [[0, 2, 4, 6, 8, 10, 12, 14], [1, 3, 5, 7, 9, 11, 13, 15]]


def shard_move(value, target):
    return lax.ppermute(value, "shard", [(s, target(s)) for s in range(16)])


def other_hi(s):
    return s ^ 8


def other_core(s):
    return s ^ 1


def up_y(s):
    return (s & 9) | ((s + 2) & 6)


def down_y(s):
    return (s & 9) | ((s - 2) & 6)


def product_kernel(acts, *refs):
    grads, out = refs[:8], refs[8]
    here = lax.axis_index("shard")
    slots = [((here >> 3) ^ far) * 4 + (((here >> 1) + up) & 3) for up in (0, 3, 1, 2) for far in (0, 1)]
    lhs = jnp.concatenate([acts[slot] for slot in slots], axis=1)
    for lane in range(0, out.shape[1], 256):
        rhs = jnp.concatenate([g[:, lane : lane + 256] for g in grads], axis=0)
        out[:, lane : lane + 256] = jnp.dot(lhs, rhs, preferred_element_type=jnp.float32).astype(out.dtype)


def product(acts, grads, flip, dtype):
    rows, cols = acts.shape[1] // 2, grads[0].shape[1]
    tokens = grads[0].shape[0]

    def half_acts():
        return (0, (lax.axis_index("shard") & 1) ^ flip, 0)

    return pl.pallas_call(
        product_kernel,
        grid=(1,),
        in_specs=[pl.BlockSpec((8, rows, tokens), lambda i: half_acts())]
        + [pl.BlockSpec((tokens, cols), lambda i: (0, 0)) for _ in grads],
        out_specs=pl.BlockSpec((rows, cols), lambda i: (0, 0)),
        out_shape=jax.ShapeDtypeStruct((rows, cols), dtype),
    )(acts, *grads)


def split_rows(block, rows, per_slot):
    at, end, out = block * rows, (block + 1) * rows, []
    while at < end:
        slot = at // per_slot
        count = min(end, (slot + 1) * per_slot) - at
        out.append((slot, at - slot * per_slot, at - block * rows, count))
        at += count
    return out


def step_kernel(first, per_slot, own, other, weights, moment, new_moment, half):
    rows, cols = other.shape
    for block in range(cols // LANES):
        here = slice(block * LANES, (block + 1) * LANES)
        there = slice((first + block) * LANES, (first + block + 1) * LANES)
        for slot, to, at, count in split_rows(block, rows, per_slot):
            band = slice(at, at + count)
            grad = own[band, here] + other[band, here].astype(jnp.float32)
            moved = (friction * moment[band, there].astype(jnp.float32) + grad).astype(jnp.bfloat16)
            new_moment[band, here] = moved
            stepped = weights[band, there].astype(jnp.float32) - step_size * moved.astype(jnp.float32)
            half[slot, to : to + count] = stepped.astype(jnp.bfloat16)


def step(own, other, weights, moment, first, slot_rows):
    rows, cols = other.shape
    per_slot = rows * cols // LANES // NODES
    return pl.pallas_call(
        functools.partial(step_kernel, first, per_slot),
        out_shape=[
            jax.ShapeDtypeStruct((rows, cols), jnp.bfloat16),
            jax.ShapeDtypeStruct((NODES, slot_rows, LANES), jnp.bfloat16),
        ],
        name="step",
    )(own, other, weights, moment)


def trim_rows(halves, at, out, to, count):

    def load(r, c):
        return halves[4 * (r % 4) + c % 4, pl.ds(at, count), :].astype(jnp.float32)

    def pair(a, b):
        return a + b, jnp.maximum(a, b), jnp.minimum(a, b)

    for rp in range(2):
        for cp in range(2):
            beside = {r: pair(load(r, cp + 1), load(r, cp + 3)) for r in (rp, rp + 2)}
            above = {c: pair(load(rp + 1, c), load(rp + 3, c)) for c in (cp, cp + 2)}
            for r in (rp, rp + 2):
                for c in (cp, cp + 2):
                    mine = load(r, c)
                    row_sum, row_max, row_min = beside[r]
                    col_sum, col_max, col_min = above[c]
                    largest = jnp.maximum(jnp.maximum(row_max, col_max), mine)
                    smallest = jnp.minimum(jnp.minimum(row_min, col_min), mine)
                    total = mine + row_sum + col_sum
                    kept = (total - largest - smallest) * (1.0 / 3.0)
                    out[4 * r + c, pl.ds(to, count), :] = kept.astype(out.dtype)


def trim_kernel(rows, halves, *refs):
    out = refs[-1]
    to = out.shape[1] - rows
    if to:
        out[:, :to] = refs[0][:, :to]
    count = 8 if rows % 16 or to % 16 else 16

    def body(i, carry):
        at = pl.multiple_of(i * count, count)
        trim_rows(halves, at, out, pl.multiple_of(at + to, count), count)
        return carry

    lax.fori_loop(0, rows // count, body, 0)


def trim(halves, rows, beside):
    shape = (NODES, rows, LANES) if beside is None else beside.shape
    extra = [] if beside is None else [beside]
    return pl.pallas_call(
        functools.partial(trim_kernel, rows),
        out_shape=jax.ShapeDtypeStruct(shape, jnp.bfloat16),
        name="trim",
    )(halves, *extra)


def assemble_kernel(*refs):
    out, lane = refs[-1], 0
    for piece in refs[:-1]:
        for b in range(piece.shape[0]):
            out[:, lane : lane + LANES] = piece[b]
            lane += LANES


def assemble(pieces, shape):
    rows = shape[0] // 4
    return pl.pallas_call(
        assemble_kernel,
        grid=(4,),
        in_specs=[pl.BlockSpec((p.shape[0], rows, LANES), lambda i: (0, i, 0)) for p in pieces],
        out_specs=pl.BlockSpec((rows, shape[1]), lambda i: (i, 0)),
        out_shape=jax.ShapeDtypeStruct(shape, jnp.bfloat16),
        name="assemble",
    )(*pieces)


def node_exchange(value):
    return lax.all_to_all(value, "node", split_axis=0, concat_axis=0)


def on_device(hidden, cotangent, weights, momentum):
    acts, grads, weights, moment = hidden[0], cotangent[0], weights[0], momentum[0]
    firsts = [sum(BLOCKS[:k]) for k in range(len(BLOCKS))]
    slot_rows = [448 * b // NODES for b in BLOCKS]

    acts = acts.T.reshape(8, 896, 128)
    acts = lax.all_to_all(acts, "shard", split_axis=0, concat_axis=0, axis_index_groups=CORE_GROUPS)

    pieces = []
    for k, blocks in enumerate(BLOCKS):
        own = grads[:, firsts[k] * LANES : (firsts[k] + blocks) * LANES]
        far = shard_move(own, other_hi)
        below_own, above_own = shard_move(own, up_y), shard_move(own, down_y)
        below_far, above_far = shard_move(far, up_y), shard_move(far, down_y)
        opposite_own = shard_move(below_own, up_y)
        opposite_far = shard_move(above_far, down_y)
        pieces.append([own, far, below_own, below_far, above_own, above_far, opposite_own, opposite_far])

    moments, exchanged, back = [], None, []
    for k in range(len(BLOCKS)):
        sent = product(acts, pieces[k], 1, jnp.bfloat16)
        other = shard_move(sent, other_core)
        own = product(acts, pieces[k], 0, jnp.float32)
        rows = slot_rows[k] + (slot_rows[k - 1] if k else 0)
        new_moment, half = step(own, other, weights, moment, firsts[k], rows)
        moments.append(new_moment)
        if k:
            half = trim(exchanged, slot_rows[k - 1], half)
        exchanged = node_exchange(half)
        if k:
            back.append(exchanged[:, slot_rows[k] :])
    last = trim(exchanged, slot_rows[-1], None)
    back.append(node_exchange(last))
    new_weights = assemble([b.reshape(-1, 448, LANES) for b in back], weights.shape)
    new_moment = jnp.concatenate(moments, axis=1)
    return new_weights[None], new_moment[None]


def solution(mesh):
    spec = P("node", "shard", None)
    return jax.shard_map(on_device, mesh=mesh, in_specs=(spec,) * 4, out_specs=(spec, spec), check_vma=False)
```

```python
import functools
import jax
import jax.numpy as jnp
from jax import lax
from jax.experimental import pallas as pl
from jax.experimental.pallas import tpu as pltpu
from jax.sharding import PartitionSpec as P

step_size = 0.1
friction = 0.9
BLOCKS = (12, 4)
NODES = 16
LANES = 128
WIDE = pltpu.CompilerParams(vmem_limit_bytes=67_000_000)
SEND_STEPS = 2
STEP_STEPS = 2
CORE_GROUPS = [[0, 2, 4, 6, 8, 10, 12, 14], [1, 3, 5, 7, 9, 11, 13, 15]]


def shard_move(value, target):
    return lax.ppermute(value, "shard", [(s, target(s)) for s in range(16)])


def other_hi(s):
    return s ^ 8


def other_core(s):
    return s ^ 1


def up_y(s):
    return (s & 9) | ((s + 2) & 6)


def down_y(s):
    return (s & 9) | ((s - 2) & 6)


def token_product(acts, grads, lane, width):
    here = lax.axis_index("shard")
    slots = [((here >> 3) ^ far) * 4 + (((here >> 1) + up) & 3) for up in (0, 3, 1, 2) for far in (0, 1)]
    lhs = jnp.concatenate([acts[slot] for slot in slots], axis=1)
    rhs = jnp.concatenate([g[:, lane : lane + width] for g in grads], axis=0)
    return jnp.dot(lhs, rhs, preferred_element_type=jnp.float32)


def half_acts(acts, flip):
    def index(i):
        return (0, (lax.axis_index("shard") & 1) ^ flip, 0)

    return pl.BlockSpec((acts.shape[0], acts.shape[1] // 2, acts.shape[2]), index)


def send_kernel(acts, *refs):
    grads, out = refs[:8], refs[8]
    for lane in range(0, out.shape[1], 256):
        out[:, lane : lane + 256] = token_product(acts, grads, lane, 256).astype(out.dtype)


def column_tile(rows, cols):
    return pl.BlockSpec((rows, cols), lambda i: (0, i))


def send_part(acts, grads):
    tokens, cols = grads[0].shape
    rows, tile = acts.shape[1] // 2, cols // SEND_STEPS
    return pl.pallas_call(
        send_kernel,
        grid=(SEND_STEPS,),
        in_specs=[half_acts(acts, 1)] + [column_tile(tokens, tile)] * 8,
        out_specs=column_tile(rows, tile),
        out_shape=jax.ShapeDtypeStruct((rows, cols), jnp.bfloat16),
        compiler_params=WIDE,
        name="send_part",
    )(acts, *grads)


def split_rows(block, rows, per_slot):
    at, end, out = block * rows, (block + 1) * rows, []
    while at < end:
        slot = at // per_slot
        count = min(end, (slot + 1) * per_slot) - at
        out.append((slot, at - slot * per_slot, at - block * rows, count))
        at += count
    return out


def spread(slots, outs):
    z = lax.axis_index("node") & 7
    for offset, out in enumerate(outs):
        out[...] = slots[(z + offset) & 7]


def step_kernel(acts, *refs):
    grads, (other, weights, moment, new_moment), rest = refs[:8], refs[8:12], refs[12:]
    half = rest[-1]
    rows, cols = other.shape
    for lane in range(0, cols, 256):
        here = slice(lane, lane + 256)
        grad = token_product(acts, grads, lane, 256) + other[:, here].astype(jnp.float32)
        moved = (friction * moment[:, here].astype(jnp.float32) + grad).astype(jnp.bfloat16)
        new_moment[:, here] = moved
        stepped = (weights[:, here].astype(jnp.float32) - step_size * moved.astype(jnp.float32)).astype(jnp.bfloat16)
        for b in range(2):
            for slot, to, at, count in split_rows(lane // LANES + b, rows, half.shape[1]):
                half[slot, to : to + count] = stepped[at : at + count, b * LANES : (b + 1) * LANES]
    if len(rest) > 1:
        spread(half, rest[:-1])


def step(acts, grads, other, weights, moment, first, apart):
    rows, cols = other.shape
    steps = 1 if apart else STEP_STEPS
    tile = cols // steps
    if first % tile:
        weights, moment, first = weights[:, first : first + cols], moment[:, first : first + cols], 0
    columns = pl.BlockSpec((rows, tile), lambda i: (0, first // tile + i))
    moved = jax.ShapeDtypeStruct((rows, cols), jnp.bfloat16)
    if apart:
        part = jax.ShapeDtypeStruct((rows * cols // LANES // 8, LANES), jnp.bfloat16)
        outs, specs = [part] * 8, [pl.BlockSpec(part.shape, lambda i: (0, 0))] * 8
        scratch = [pltpu.VMEM((8, *part.shape), jnp.bfloat16)]
    else:
        outs = [jax.ShapeDtypeStruct((cols // LANES, rows, LANES), jnp.bfloat16)]
        specs = [pl.BlockSpec((tile // LANES, rows, LANES), lambda i: (i, 0, 0))]
        scratch = []
    new_moment, *half = pl.pallas_call(
        step_kernel,
        grid=(steps,),
        in_specs=[half_acts(acts, 0)]
        + [column_tile(grads[0].shape[0], tile)] * 8
        + [column_tile(rows, tile), columns, columns],
        out_specs=[column_tile(rows, tile)] + specs,
        out_shape=[moved] + outs,
        scratch_shapes=scratch,
        compiler_params=WIDE,
        name="step",
    )(acts, *grads, other, weights, moment)
    return new_moment, half if apart else half[0].reshape(NODES, -1, LANES)


def pair(a, b):
    return a + b, jnp.maximum(a, b), jnp.minimum(a, b)


def trimmed(mine, one, two):
    one_sum, one_max, one_min = one
    two_sum, two_max, two_min = two
    largest = jnp.maximum(jnp.maximum(one_max, two_max), mine)
    smallest = jnp.minimum(jnp.minimum(one_min, two_min), mine)
    return ((mine + one_sum + two_sum - largest - smallest) * (1.0 / 3.0)).astype(jnp.bfloat16)


def over_rows(rows, body):
    count = 8 if rows % 16 else 16

    def one(i, carry):
        body(pl.ds(pl.multiple_of(i * count, count), count))
        return carry

    lax.fori_loop(0, rows // count, one, 0)


def trim_kernel(halves, out):
    def body(at):
        def load(r, c):
            return halves[4 * (r % 4) + c % 4, at, :].astype(jnp.float32)

        for rp in range(2):
            for cp in range(2):
                beside = {r: pair(load(r, cp + 1), load(r, cp + 3)) for r in (rp, rp + 2)}
                above = {c: pair(load(rp + 1, c), load(rp + 3, c)) for c in (cp, cp + 2)}
                for r in (rp, rp + 2):
                    for c in (cp, cp + 2):
                        out[4 * r + c, at, :] = trimmed(load(r, c), beside[r], above[c])

    over_rows(halves.shape[1], body)


def trim(halves):
    tile = halves.shape[1] if halves.shape[1] % 112 else 112
    spec = pl.BlockSpec((NODES, tile, LANES), lambda i: (0, i, 0))
    return pl.pallas_call(
        trim_kernel,
        grid=(halves.shape[1] // tile,),
        in_specs=[spec],
        out_specs=spec,
        out_shape=jax.ShapeDtypeStruct(halves.shape, jnp.bfloat16),
        compiler_params=WIDE,
        name="trim",
    )(halves)


def trim_apart_kernel(*refs):
    outs, (near, far, result) = refs[16:24], refs[24:]
    z = lax.axis_index("node") & 7
    for offset in range(8):
        near[(z - offset) & 7] = refs[offset][...]
        far[(z - offset) & 7] = refs[8 + offset][...]

    def body(at):
        def load(ref, r, c):
            return ref[4 * r + c % 4, at, :].astype(jnp.float32)

        for r in range(2):
            for cp in range(2):
                beside = pair(load(near, r, cp + 1), load(near, r, cp + 3))
                for c in (cp, cp + 2):
                    above = pair(load(near, 1 - r, c), load(far, 1 - r, c))
                    result[4 * r + c, at, :] = trimmed(load(near, r, c), beside, above)

    over_rows(near.shape[1], body)
    spread(result, outs)


def trim_apart(near, far):
    rows = near[0].shape[0]
    tile = 112 if rows % 224 else 224
    out = jax.ShapeDtypeStruct((rows, LANES), jnp.bfloat16)
    spec = pl.BlockSpec((tile, LANES), lambda i: (i, 0))
    return pl.pallas_call(
        trim_apart_kernel,
        grid=(rows // tile,),
        in_specs=[spec] * 16,
        out_specs=[spec] * 8,
        out_shape=[out] * 8,
        scratch_shapes=[pltpu.VMEM((8, tile, LANES), jnp.bfloat16)] * 3,
        compiler_params=WIDE,
        name="trim_apart",
    )(*near, *far)


ANY = pl.BlockSpec(memory_space=pl.ANY)


def copy_all(pairs, sems):
    copies = [pltpu.make_async_copy(source, target, sems.at[i]) for i, (source, target) in enumerate(pairs)]
    for copy in copies:
        copy.start()
    for copy in copies:
        copy.wait()


def lay_kernel(piece, out, sems):
    copy_all([(piece.at[b], out.at[:, pl.ds(b * LANES, LANES)]) for b in range(piece.shape[0])], sems)


def lay(piece, shape):
    return pl.pallas_call(
        lay_kernel,
        in_specs=[pl.BlockSpec(memory_space=pltpu.VMEM)],
        out_specs=ANY,
        out_shape=jax.ShapeDtypeStruct(shape, jnp.bfloat16),
        scratch_shapes=[pltpu.SemaphoreType.DMA((piece.shape[0],))],
        compiler_params=WIDE,
        name="lay",
    )(piece)


def lay_apart_kernel(first, laid, *refs):
    del laid
    pieces, out, sems = refs[:8], refs[8], refs[9]
    z = lax.axis_index("node") & 7
    parts = pieces[0].shape[0] // 112
    pairs = []
    for offset, piece in enumerate(pieces):
        for part in range(parts):
            spot = ((z - offset) & 7) * parts + part
            lane = pl.multiple_of((first + (spot >> 2)) * LANES, LANES)
            row = pl.multiple_of((spot & 3) * 112, 16)
            pairs.append((piece.at[pl.ds(part * 112, 112)], out.at[pl.ds(row, 112), pl.ds(lane, LANES)]))
    copy_all(pairs, sems)


def lay_apart(laid, pieces, first):
    return pl.pallas_call(
        functools.partial(lay_apart_kernel, first),
        in_specs=[ANY] + [pl.BlockSpec(memory_space=pltpu.VMEM)] * 8,
        out_specs=ANY,
        out_shape=jax.ShapeDtypeStruct(laid.shape, jnp.bfloat16),
        scratch_shapes=[pltpu.SemaphoreType.DMA((8 * pieces[0].shape[0] // 112,))],
        input_output_aliases={0: 0},
        compiler_params=WIDE,
        name="lay_apart",
    )(laid, *pieces)


ORDER = (4, 5, 3, 6, 2, 7, 1)


def ring_exchange(pieces):
    got = {0: pieces[0]}
    for offset in ORDER:
        pairs = [(n, (n & 8) | ((n + offset) & 7)) for n in range(NODES)]
        got[offset] = lax.ppermute(pieces[offset], "node", pairs)
    return [got[offset] for offset in range(8)]


def node_exchange(value):
    return lax.all_to_all(value, "node", split_axis=0, concat_axis=0)


def on_device(hidden, cotangent, weights, momentum):
    acts, grads, weights, moment = hidden[0], cotangent[0], weights[0], momentum[0]
    cuts = [slice(0, BLOCKS[0] * LANES), slice(BLOCKS[0] * LANES, grads.shape[1])]

    acts = acts.T.reshape(8, 896, 128)
    acts = lax.all_to_all(acts, "shard", split_axis=0, concat_axis=0, axis_index_groups=CORE_GROUPS)

    pieces = []
    for cut in cuts:
        own = grads[:, cut]
        far = shard_move(own, other_hi)
        below_own, above_own = shard_move(own, up_y), shard_move(own, down_y)
        below_far, above_far = shard_move(far, up_y), shard_move(far, down_y)
        opposite_own = shard_move(below_own, up_y)
        opposite_far = shard_move(above_far, down_y)
        pieces.append([own, far, below_own, below_far, above_own, above_far, opposite_own, opposite_far])

    moments, halves = [], []
    for k, cut in enumerate(cuts):
        sent = send_part(acts, pieces[k])
        other = shard_move(sent, other_core)
        new_moment, half = step(acts, pieces[k], other, weights, moment, cut.start, k == 1)
        moments.append(new_moment)
        halves.append(half)

    exchanged = node_exchange(halves[0])
    result = trim(exchanged)
    returned = node_exchange(result)
    laid = lay(returned.reshape(-1, 448, LANES), weights.shape)

    near = ring_exchange(halves[1])
    far = []
    for piece in near:
        far.append(lax.ppermute(piece, "node", [(n, n ^ 8) for n in range(NODES)]))
    results = trim_apart(near, far)
    arrived = ring_exchange(results)
    new_weights = lay_apart(laid, arrived, BLOCKS[0])
    new_moment = jnp.concatenate(moments, axis=1)
    return new_weights[None], new_moment[None]


def solution(mesh):
    spec = P("node", "shard", None)
    return jax.shard_map(on_device, mesh=mesh, in_specs=(spec,) * 4, out_specs=(spec, spec), check_vma=False)
```

```python
import functools
import jax
import jax.numpy as jnp
from jax import lax
from jax.experimental import pallas as pl
from jax.experimental.pallas import tpu as pltpu
from jax.sharding import PartitionSpec as P

step_size = 0.1
friction = 0.9
BLOCKS = (12, 4)
NODES = 16
LANES = 128
WIDE = pltpu.CompilerParams(vmem_limit_bytes=67_000_000)
SEND_STEPS = 2
STEP_STEPS = 2
CORE_GROUPS = [[0, 2, 4, 6, 8, 10, 12, 14], [1, 3, 5, 7, 9, 11, 13, 15]]


def shard_move(value, target):
    return lax.ppermute(value, "shard", [(s, target(s)) for s in range(16)])


def other_hi(s):
    return s ^ 8


def other_core(s):
    return s ^ 1


def up_y(s):
    return (s & 9) | ((s + 2) & 6)


def down_y(s):
    return (s & 9) | ((s - 2) & 6)


def token_product(acts, grads, lane, width):
    here = lax.axis_index("shard")
    slots = [((here >> 3) ^ far) * 4 + (((here >> 1) + up) & 3) for up in (0, 3, 1, 2) for far in (0, 1)]
    lhs = jnp.concatenate([acts[slot] for slot in slots], axis=1)
    rhs = jnp.concatenate([g[:, lane : lane + width] for g in grads], axis=0)
    return jnp.dot(lhs, rhs, preferred_element_type=jnp.float32)


def half_acts(acts, flip):
    def index(i):
        return (0, (lax.axis_index("shard") & 1) ^ flip, 0)

    return pl.BlockSpec((acts.shape[0], acts.shape[1] // 2, acts.shape[2]), index)


def send_kernel(acts, *refs):
    grads, out = refs[:8], refs[8]
    for lane in range(0, out.shape[1], 256):
        out[:, lane : lane + 256] = token_product(acts, grads, lane, 256).astype(out.dtype)


def column_tile(rows, cols, spot=0):
    return pl.BlockSpec((rows, cols), lambda i: (0, spot + i))


def send_part(acts, mine, grads, first):
    tokens, cols = grads[0].shape
    rows, tile = acts.shape[1] // 2, cols // SEND_STEPS
    return pl.pallas_call(
        send_kernel,
        grid=(SEND_STEPS,),
        in_specs=[half_acts(acts, 1), column_tile(tokens, tile, first // tile)] + [column_tile(tokens, tile)] * 7,
        out_specs=column_tile(rows, tile),
        out_shape=jax.ShapeDtypeStruct((rows, cols), jnp.bfloat16),
        compiler_params=WIDE,
        name="send_part",
    )(acts, mine, *grads)


def split_rows(block, rows, per_slot):
    at, end, out = block * rows, (block + 1) * rows, []
    while at < end:
        slot = at // per_slot
        count = min(end, (slot + 1) * per_slot) - at
        out.append((slot, at - slot * per_slot, at - block * rows, count))
        at += count
    return out


def spread(slots, outs):
    z = lax.axis_index("node") & 7
    for offset, out in enumerate(outs):
        out[...] = slots[(z + offset) & 7]


def step_kernel(carried, acts, *refs):
    grads, (other, weights, moment), rest = refs[:8], refs[8:11], refs[11 + carried :]
    new_moment, rest = rest[0], rest[1:]
    half = rest[-1]
    rows, cols = other.shape
    for lane in range(0, cols, 256):
        here = slice(lane, lane + 256)
        grad = token_product(acts, grads, lane, 256) + other[:, here].astype(jnp.float32)
        moved = (friction * moment[:, here].astype(jnp.float32) + grad).astype(jnp.bfloat16)
        new_moment[:, here] = moved
        stepped = (weights[:, here].astype(jnp.float32) - step_size * moved.astype(jnp.float32)).astype(jnp.bfloat16)
        for b in range(2):
            for slot, to, at, count in split_rows(lane // LANES + b, rows, half.shape[1]):
                half[slot, to : to + count] = stepped[at : at + count, b * LANES : (b + 1) * LANES]
    if len(rest) > 1:
        spread(half, rest[:-1])


def step(acts, mine, grads, other, weights, moment, first, new_moment, apart):
    rows, cols = other.shape
    steps = 1 if apart else STEP_STEPS
    tile = cols // steps
    columns = pl.BlockSpec((rows, tile), lambda i: (0, first // tile + i))
    moved = jax.ShapeDtypeStruct(weights.shape, jnp.bfloat16)
    carried = [] if new_moment is None else [new_moment]
    if apart:
        part = jax.ShapeDtypeStruct((rows * cols // LANES // 8, LANES), jnp.bfloat16)
        outs, specs = [part] * 8, [pl.BlockSpec(part.shape, lambda i: (0, 0))] * 8
        scratch = [pltpu.VMEM((8, *part.shape), jnp.bfloat16)]
    else:
        outs = [jax.ShapeDtypeStruct((cols // LANES, rows, LANES), jnp.bfloat16)]
        specs = [pl.BlockSpec((tile // LANES, rows, LANES), lambda i: (i, 0, 0))]
        scratch = []
    new_moment, *half = pl.pallas_call(
        functools.partial(step_kernel, len(carried)),
        grid=(steps,),
        in_specs=[half_acts(acts, 0), column_tile(mine.shape[0], tile, first // tile)]
        + [column_tile(mine.shape[0], tile)] * 7
        + [column_tile(rows, tile), columns, columns]
        + [pl.BlockSpec(memory_space=pl.ANY)] * len(carried),
        out_specs=[columns] + specs,
        out_shape=[moved] + outs,
        scratch_shapes=scratch,
        input_output_aliases={12: 0} if carried else {},
        compiler_params=WIDE,
        name="step",
    )(acts, mine, *grads, other, weights, moment, *carried)
    return new_moment, half if apart else half[0].reshape(NODES, -1, LANES)


def pair(a, b):
    return a + b, jnp.maximum(a, b), jnp.minimum(a, b)


def trimmed(mine, one, two):
    one_sum, one_max, one_min = one
    two_sum, two_max, two_min = two
    largest = jnp.maximum(jnp.maximum(one_max, two_max), mine)
    smallest = jnp.minimum(jnp.minimum(one_min, two_min), mine)
    return ((mine + one_sum + two_sum - largest - smallest) * (1.0 / 3.0)).astype(jnp.bfloat16)


def over_rows(rows, body):
    count = 8 if rows % 16 else 16

    def one(i, carry):
        body(pl.ds(pl.multiple_of(i * count, count), count))
        return carry

    lax.fori_loop(0, rows // count, one, 0)


def trim_kernel(halves, out):
    def body(at):
        def load(r, c):
            return halves[4 * (r % 4) + c % 4, at, :].astype(jnp.float32)

        for rp in range(2):
            for cp in range(2):
                beside = {r: pair(load(r, cp + 1), load(r, cp + 3)) for r in (rp, rp + 2)}
                above = {c: pair(load(rp + 1, c), load(rp + 3, c)) for c in (cp, cp + 2)}
                for r in (rp, rp + 2):
                    for c in (cp, cp + 2):
                        out[4 * r + c, at, :] = trimmed(load(r, c), beside[r], above[c])

    over_rows(halves.shape[1], body)


def trim(halves):
    tile = halves.shape[1] // 2
    spec = pl.BlockSpec((NODES, tile, LANES), lambda i: (0, i, 0))
    return pl.pallas_call(
        trim_kernel,
        grid=(halves.shape[1] // tile,),
        in_specs=[spec],
        out_specs=spec,
        out_shape=jax.ShapeDtypeStruct(halves.shape, jnp.bfloat16),
        compiler_params=WIDE,
        name="trim",
    )(halves)


def trim_apart_kernel(*refs):
    outs, (near, far, result) = refs[16:24], refs[24:]
    z = lax.axis_index("node") & 7
    for offset in range(8):
        near[(z - offset) & 7] = refs[offset][...]
        far[(z - offset) & 7] = refs[8 + offset][...]

    def body(at):
        def load(ref, r, c):
            return ref[4 * r + c % 4, at, :].astype(jnp.float32)

        for r in range(2):
            for cp in range(2):
                beside = pair(load(near, r, cp + 1), load(near, r, cp + 3))
                for c in (cp, cp + 2):
                    above = pair(load(near, 1 - r, c), load(far, 1 - r, c))
                    result[4 * r + c, at, :] = trimmed(load(near, r, c), beside, above)

    over_rows(near.shape[1], body)
    spread(result, outs)


def trim_apart(near, far):
    rows = near[0].shape[0]
    tile = 112 if rows % 224 else 224
    out = jax.ShapeDtypeStruct((rows, LANES), jnp.bfloat16)
    spec = pl.BlockSpec((tile, LANES), lambda i: (i, 0))
    return pl.pallas_call(
        trim_apart_kernel,
        grid=(rows // tile,),
        in_specs=[spec] * 16,
        out_specs=[spec] * 8,
        out_shape=[out] * 8,
        scratch_shapes=[pltpu.VMEM((8, tile, LANES), jnp.bfloat16)] * 3,
        name="trim_apart",
    )(*near, *far)


ANY = pl.BlockSpec(memory_space=pl.ANY)


def copy_all(pairs, sems):
    copies = [pltpu.make_async_copy(source, target, sems.at[i]) for i, (source, target) in enumerate(pairs)]
    for copy in copies:
        copy.start()
    for copy in copies:
        copy.wait()


def lay_kernel(piece, out, sems):
    copy_all([(piece.at[b], out.at[:, pl.ds(b * LANES, LANES)]) for b in range(piece.shape[0])], sems)


def lay(piece, shape):
    return pl.pallas_call(
        lay_kernel,
        in_specs=[pl.BlockSpec(memory_space=pltpu.VMEM)],
        out_specs=ANY,
        out_shape=jax.ShapeDtypeStruct(shape, jnp.bfloat16),
        scratch_shapes=[pltpu.SemaphoreType.DMA((piece.shape[0],))],
        compiler_params=WIDE,
        name="lay",
    )(piece)


def lay_apart_kernel(first, laid, *refs):
    del laid
    pieces, out, sems = refs[:8], refs[8], refs[9]
    z = lax.axis_index("node") & 7
    parts = pieces[0].shape[0] // 112
    pairs = []
    for offset, piece in enumerate(pieces):
        for part in range(parts):
            spot = ((z - offset) & 7) * parts + part
            lane = pl.multiple_of((first + (spot >> 2)) * LANES, LANES)
            row = pl.multiple_of((spot & 3) * 112, 16)
            pairs.append((piece.at[pl.ds(part * 112, 112)], out.at[pl.ds(row, 112), pl.ds(lane, LANES)]))
    copy_all(pairs, sems)


def lay_apart(laid, pieces, first):
    return pl.pallas_call(
        functools.partial(lay_apart_kernel, first),
        in_specs=[ANY] + [pl.BlockSpec(memory_space=pltpu.VMEM)] * 8,
        out_specs=ANY,
        out_shape=jax.ShapeDtypeStruct(laid.shape, jnp.bfloat16),
        scratch_shapes=[pltpu.SemaphoreType.DMA((8 * pieces[0].shape[0] // 112,))],
        input_output_aliases={0: 0},
        compiler_params=WIDE,
        name="lay_apart",
    )(laid, *pieces)


def ring_exchange(pieces):
    got = {0: pieces[0]}
    for offset in range(1, 8):
        pairs = [(n, (n & 8) | ((n + offset) & 7)) for n in range(NODES)]
        got[offset] = lax.ppermute(pieces[offset], "node", pairs)
    return [got[offset] for offset in range(8)]


def node_exchange(value):
    return lax.all_to_all(value, "node", split_axis=0, concat_axis=0)


def on_device(hidden, cotangent, weights, momentum):
    acts, grads, weights, moment = hidden[0], cotangent[0], weights[0], momentum[0]
    cuts = [slice(0, BLOCKS[0] * LANES), slice(BLOCKS[0] * LANES, grads.shape[1])]

    acts = acts.T.reshape(8, 896, 128)
    acts = lax.all_to_all(acts, "shard", split_axis=0, concat_axis=0, axis_index_groups=CORE_GROUPS)

    pieces = []
    for cut in cuts:
        own = grads[:, cut]
        far = shard_move(own, other_hi)
        below_own, above_own = shard_move(own, up_y), shard_move(own, down_y)
        below_far, above_far = shard_move(far, up_y), shard_move(far, down_y)
        opposite_own = shard_move(below_own, up_y)
        opposite_far = shard_move(above_far, down_y)
        pieces.append([far, below_own, below_far, above_own, above_far, opposite_own, opposite_far])

    new_moment, halves = None, []
    for k, cut in enumerate(cuts):
        sent = send_part(acts, grads, pieces[k], cut.start)
        other = shard_move(sent, other_core)
        new_moment, half = step(acts, grads, pieces[k], other, weights, moment, cut.start, new_moment, k == 1)
        halves.append(half)

    exchanged = node_exchange(halves[0])
    result = trim(exchanged)
    returned = node_exchange(result)
    laid = lay(returned.reshape(-1, 448, LANES), weights.shape)

    near = ring_exchange(halves[1])
    far = []
    for piece in near:
        far.append(lax.ppermute(piece, "node", [(n, n ^ 8) for n in range(NODES)]))
    results = trim_apart(near, far)
    arrived = ring_exchange(results)
    new_weights = lay_apart(laid, arrived, BLOCKS[0])
    return new_weights[None], new_moment[None]


def solution(mesh):
    spec = P("node", "shard", None)
    return jax.shard_map(on_device, mesh=mesh, in_specs=(spec,) * 4, out_specs=(spec, spec), check_vma=False)
```
